32 devices in a mesh: dp: 4 (over z), ctx: 8 (over y, x, core).
Axes of the slice: x: 2, y: 2, z: 4, core: 2. Of those that a mesh axis runs over, the one named last changes fastest.
Arguments:
- queries: bfloat16 [4, 1024, 1024], P('dp', 'ctx'), may hold values from -6 to 6
- keys: bfloat16 [4, 1024, 1024], P('dp', 'ctx'), may hold values from -6 to 6
- values: bfloat16 [4, 1024, 1024], P('dp', 'ctx'), may hold values from -6 to 6
- outputs: bfloat16 [4, 1024, 1024], P('dp', 'ctx'), may hold values from -1.25 to 1.25
- d_out: bfloat16 [4, 1024, 1024], P('dp', 'ctx'), may hold values from -6 to 6
- lse: float32 [4, 16, 1024], P('dp', None, 'ctx'), may hold values from 3 to 5
- glob_keys: bfloat16 [128, 1024], replicated, may hold values from -6 to 6
- glob_values: bfloat16 [128, 1024], replicated, may hold values from -6 to 6
- rand_owner: int32 [16, 3], P('ctx'), may hold values from 0 to 7, all different within a row; in each aligned block of 2 rows (0 to 1, 2 to 3, ...) at most 2 rows name the same one
- rand_local: int32 [16, 3], P('ctx'), may hold values from 0 to 1
Outputs:
- d_queries: bfloat16 [4, 1024, 1024], P('dp', 'ctx')
- d_keys: bfloat16 [4, 1024, 1024], P('dp', 'ctx')
- d_values: bfloat16 [4, 1024, 1024], P('dp', 'ctx')
- d_glob_keys: float32 [128, 1024], replicated
- d_glob_values: float32 [128, 1024], replicated
The draws below stay inside these ranges and needn't reach their ends.
Inputs may be any that keep to these rules, and one draw needn't show every extreme that they name: `rand_owner`: the 3 random blocks of one query block lie on different ctx indices. Among the 2 query blocks of one device no ctx index is named more than 2 times.
All inputs are finite; a program needn't handle non-finite values.
Results may differ from the reference program's by a relative error of at most 0.0055.
Values may be sent and summed in bfloat16 or wider, within the bound.
A program may use at most 128 MiB of HBM per device.

```python
import math
import jax
import jax.numpy as jnp
import numpy as np
from jax import lax

HEADS = 16
HDIM = 64
BLK = 64
R_BLK = 3
NB_DEV = 2
D = 1024
GLOB = 128
SEQ = 1024
NBLK = 16
GENOMES = 4
CAP = 2
N_CTX = 8


def with_ends(entries, own_key, low, high):
    extent = entries.shape
    spot = [jax.random.randint(jax.random.fold_in(own_key, axis), (), 0, extent[axis]) for axis in range(len(extent))]
    entries = entries.at[tuple(spot)].set(low)
    longest = extent.index(max(extent))
    spot[longest] = (spot[longest] + 1) % extent[longest]
    return entries.at[tuple(spot)].set(high)


def shard_levels(stream_key, extent, shards, smallest, top_value):
    factor_of = 1.0
    for axis_at, parts in shards:
        heights = jax.random.uniform(jax.random.fold_in(jax.random.fold_in(stream_key, 6), axis_at), (parts,), jnp.float32, smallest / len(shards), top_value / len(shards))
        factor_of = factor_of * jnp.repeat(jnp.exp(heights), extent[axis_at] // parts).reshape((-1,) + (1,) * (len(extent) - 1 - axis_at))
    return factor_of


def routed_block(rng, own, number, rows, amount, top, limit, slope):
    sequence = jax.random.permutation(rng, amount)
    crowded, ordinary = portions_of(amount, rows * top, limit, slope, True), portions_of(amount, rows * top, limit, slope, False)
    places = jnp.arange(amount)

    def named(sizes, rotation):
        used = int((sizes > 0).sum())
        fixed = max(1, used // 4)
        passed = fixed + (places - fixed + rotation * (used - fixed)) % max(1, amount - fixed)
        return jnp.zeros((amount,), jnp.int32).at[sequence[jnp.where(places < fixed, places, passed)]].set(jnp.asarray(sizes, jnp.int32))

    sizes = jnp.where(number % 4 == 0, named(crowded, number // 4), named(ordinary, number - number // 4 - 1))
    mixed = jax.random.permutation(jax.random.fold_in(own, 3), amount)
    source_of, taker = mixed[0:amount // 2 * 2:2], mixed[1:amount // 2 * 2:2]
    margin = jnp.minimum(sizes[source_of] - 1, limit - sizes[taker]) // 2
    margin = jnp.where((source_of == sequence[0]) | (taker == sequence[0]) | (sizes[taker] == 0), 0, jnp.maximum(margin, 0))
    passed = jax.random.randint(jax.random.fold_in(own, 4), (amount // 2,), 0, 1 << 20) % (margin + 1)
    sizes = sizes.at[source_of].add(-passed).at[taker].add(passed)
    labels = jnp.searchsorted(jnp.cumsum(sizes), jnp.arange(rows * top), side="right").astype(jnp.int32)
    listing = labels.reshape(top, rows).T
    listing = listing[jax.random.permutation(jax.random.fold_in(own, 1), rows)]
    rotation = jax.random.randint(jax.random.fold_in(own, 2), (rows, 1), 0, top)
    return jnp.take_along_axis(listing, (jnp.arange(top)[None, :] + rotation) % top, axis=1)


def portions_of(number_of, total, most, skew, full):
    portions = [(1 << 20) // math.isqrt(standing ** skew) + 1 for standing in range(1, number_of + 1)]
    largest = most if full else min(most, max(-(-total // number_of), total * portions[0] // sum(portions)))
    least = 1 if total - largest >= number_of - 1 else 0
    counts, spare = [largest] + [least] * (number_of - 1), total - largest - least * (number_of - 1)
    while spare > 0:
        free = [i for i in range(1, number_of) if counts[i] < largest] or [i for i in range(1, number_of) if counts[i] < most]
        whole, remaining = sum([portions[i] for i in free]), spare
        for i in free:
            more = min(most - counts[i], max(1, remaining * portions[i] // whole), spare)
            counts[i] = counts[i] + more
            spare = spare - more
    return np.array(counts)


def normal_values(key, extent, width, most, pieces=(), kind=jnp.bfloat16):
    values = width * jax.random.normal(key, extent, jnp.float32)
    if pieces:
        values = values * shard_levels(key, extent, pieces, -0.22, 0.18)
    return jnp.clip(values, -most, most).astype(kind)


def setup_inputs(seed: int = 0) -> dict:
    key_of = jax.random.split(jax.random.key(seed), 11)
    queries = normal_values(key_of[0], (GENOMES, SEQ, D), 1.0, 6.0, ((0, 4), (1, 8)))
    keys = normal_values(key_of[1], (GENOMES, SEQ, D), 1.0, 6.0, ((0, 4), (1, 8)))
    values = normal_values(key_of[2], (GENOMES, SEQ, D), 1.0, 6.0, ((0, 4), (1, 8)))
    outputs = normal_values(key_of[3], (GENOMES, SEQ, D), 0.2, 1.25, ((0, 4), (1, 8)))
    d_out = normal_values(key_of[4], (GENOMES, SEQ, D), 1.0, 6.0, ((0, 4), (1, 8)))
    lse = jnp.clip(3.0 + 2.0 * jax.random.uniform(key_of[5], (GENOMES, HEADS, SEQ), jnp.float32) ** shard_levels(key_of[5], (GENOMES, HEADS, SEQ), ((0, 4), (2, 8)), -0.2, 0.2), 3.0, 5.0)
    glob_keys = normal_values(key_of[6], (GLOB, D), 1.0, 6.0)
    glob_values = normal_values(key_of[7], (GLOB, D), 1.0, 6.0)
    rand_owner_keys = jax.random.split(jax.random.fold_in(key_of[8], 1), NBLK // NB_DEV)
    rand_owner_turns = jax.random.permutation(jax.random.fold_in(key_of[8], 3), NBLK // NB_DEV)
    rand_owner = jax.vmap(lambda own, number: routed_block(jax.random.fold_in(key_of[8], 2), own, number, NB_DEV, N_CTX, R_BLK, CAP, 2))(rand_owner_keys, rand_owner_turns).reshape((NBLK, R_BLK))
    rand_local = with_ends(jax.random.randint(key_of[9], (NBLK, R_BLK), 0, NB_DEV), jax.random.fold_in(key_of[9], 1), 0, NB_DEV - 1).astype(jnp.int32)
    return dict(queries=queries, keys=keys, values=values, outputs=outputs, d_out=d_out, lse=lse, glob_keys=glob_keys, glob_values=glob_values, rand_owner=rand_owner, rand_local=rand_local)


def rounded(tensor):
    return lax.optimization_barrier(tensor.astype(jnp.bfloat16)).astype(jnp.float32)


def block_grads(query_blk, dout_blk, lse_blk, delta_blk, key_blk, value_blk):
    scaling = HDIM ** -0.5
    query_f = query_blk.astype(jnp.float32)
    dout_f = dout_blk.astype(jnp.float32)
    key_f = key_blk.astype(jnp.float32)
    value_f = value_blk.astype(jnp.float32)
    scores = jnp.einsum('nqhe,nkhe->nhqk', query_f, key_f) * scaling
    probability = jnp.exp(scores - lse_blk[..., None])
    prob_low = rounded(probability)
    d_probability = jnp.einsum('nqhe,nkhe->nhqk', dout_f, value_f)
    d_scores = rounded(probability * (d_probability - delta_blk[..., None]))
    grad_q = jnp.einsum('nhqk,nkhe->nqhe', d_scores, key_f) * scaling
    grad_k = jnp.einsum('nhqk,nqhe->nkhe', d_scores, query_f) * scaling
    grad_v = jnp.einsum('nhqk,nqhe->nkhe', prob_low, dout_f)
    return grad_q, grad_k, grad_v


def one_genome(queries, keys, values, outputs, d_out, lse, glob_keys, glob_values, rand_owner, rand_local):
    query_blk = queries.reshape(NBLK, BLK, HEADS, HDIM)
    key_blk = keys.reshape(NBLK, BLK, HEADS, HDIM)
    value_blk = values.reshape(NBLK, BLK, HEADS, HDIM)
    dout_blk = d_out.reshape(NBLK, BLK, HEADS, HDIM)
    product = d_out.astype(jnp.float32) * outputs.astype(jnp.float32)
    delta_blk = jnp.sum(product.reshape(NBLK, BLK, HEADS, HDIM), axis=3).transpose(0, 2, 1)
    lse_blk = lse.astype(jnp.float32).reshape(HEADS, NBLK, BLK).transpose(1, 0, 2)
    key_win = jnp.concatenate([jnp.roll(key_blk, 1, 0), key_blk, jnp.roll(key_blk, -1, 0)], axis=1)
    value_win = jnp.concatenate([jnp.roll(value_blk, 1, 0), value_blk, jnp.roll(value_blk, -1, 0)], axis=1)
    dq_win, dk_win, dv_win = block_grads(query_blk, dout_blk, lse_blk, delta_blk, key_win, value_win)

    def fold_window(section):
        return jnp.roll(section[:, :BLK], -1, 0) + section[:, BLK:2 * BLK] + jnp.roll(section[:, 2 * BLK:], 1, 0)

    grad_keys = fold_window(dk_win)
    grad_values = fold_window(dv_win)
    mem_keys = jnp.broadcast_to(glob_keys.reshape(1, GLOB, HEADS, HDIM), (NBLK, GLOB, HEADS, HDIM))
    mem_values = jnp.broadcast_to(glob_values.reshape(1, GLOB, HEADS, HDIM), (NBLK, GLOB, HEADS, HDIM))
    dq_mem, dk_mem, dv_mem = block_grads(query_blk, dout_blk, lse_blk, delta_blk, mem_keys, mem_values)
    grad_queries = dq_win + dq_mem
    for column in range(R_BLK):
        key_index = (rand_owner[:, column] * NB_DEV + rand_local[:, column]).astype(jnp.int32)
        dq_rand, dk_rand, dv_rand = block_grads(query_blk, dout_blk, lse_blk, delta_blk, key_blk[key_index], value_blk[key_index])
        grad_queries = grad_queries + rounded(dq_rand)
        grad_keys = grad_keys + jax.ops.segment_sum(rounded(dk_rand), key_index, num_segments=NBLK)
        grad_values = grad_values + jax.ops.segment_sum(rounded(dv_rand), key_index, num_segments=NBLK)
    return (grad_queries.reshape(SEQ, D).astype(jnp.bfloat16),
            grad_keys.reshape(SEQ, D).astype(jnp.bfloat16),
            grad_values.reshape(SEQ, D).astype(jnp.bfloat16),
            jnp.sum(dk_mem, axis=0).reshape(GLOB, D),
            jnp.sum(dv_mem, axis=0).reshape(GLOB, D))


def reference(queries, keys, values, outputs, d_out, lse, glob_keys, glob_values, rand_owner, rand_local):
    def genome_step(totals, genome_items):
        grad_q, grad_k, grad_v, mem_k, mem_v = one_genome(*genome_items, glob_keys, glob_values, rand_owner, rand_local)
        return (totals[0] + mem_k, totals[1] + mem_v), (grad_q, grad_k, grad_v)

    zeros_init = jnp.zeros((GLOB, D), jnp.float32)
    totals, grads = lax.scan(genome_step, (zeros_init, zeros_init), (queries, keys, values, outputs, d_out, lse))
    return (grads[0], grads[1], grads[2], totals[0], totals[1])
```

```python
import functools

import jax
import jax.numpy as jnp
from jax import lax
from jax.experimental import pallas as pl
from jax.experimental.pallas import tpu as pltpu
from jax.sharding import PartitionSpec as P

HEADS = 16
HDIM = 64
BLK = 64
GLOB = 128
NONE = -1e30
MESH = pl.DeviceIdType.MESH
F32 = jnp.float32
BF16 = jnp.bfloat16
NT = (((1,), (1,)), ((), ()))
NN = (((1,), (0,)), ((), ()))
Q, DO, SIDE, K, V, DK, DV, DQ, MEM = range(9)


def dot(a, b, dims):
    return lax.dot_general(a, b, dims, preferred_element_type=F32)


def kernel(
    n, n_dp, tokens, width, direct,
    owner_ref, local_ref, q_ref, k_ref, v_ref, o_ref, do_ref, lse_ref, gk_ref, gv_ref,
    dq_ref, dk_ref, dv_ref, dgk_ref, dgv_ref,
    q_all, do_all, k_all, v_all, side_out, side_all, dq_out, dk_out, dv_out, dq_sum,
    mem_out, mem_dp, tot_out, tot_all,
    send, recv, dp_send, dp_recv,
):
    me = lax.axis_index("ctx")
    me_dp = lax.axis_index("dp")
    heads = width // HDIM
    blocks = tokens // BLK
    total = n * blocks
    per_block = owner_ref.shape[1]
    scale = HDIM ** (-0.5)

    def peer(i):
        return lax.rem(me + i, n)

    def source(i):
        return lax.rem(me + n - i, n)

    def peer_dp(i):
        return lax.rem(me_dp + i, n_dp)

    def cols(ref, d):
        if direct:
            return ref.at[:, pl.ds(pl.multiple_of(d * width, width), width)]
        return ref.at[d]

    def rows(ref, d):
        return ref.at[pl.ds(pl.multiple_of(d * tokens, tokens), tokens), :]

    def lanes(ref, d):
        return ref.at[:, pl.ds(pl.multiple_of(d * tokens, tokens), tokens)]

    def remote(kind, src, dst, i, d):
        return pltpu.make_async_remote_copy(
            src_ref=src,
            dst_ref=dst,
            send_sem=send.at[kind, i],
            recv_sem=recv.at[kind, i],
            device_id={"ctx": d},
            device_id_type=MESH,
        )

    def incoming(kind, src_ref, all_ref, i):
        d = peer(i)
        return remote(kind, cols(src_ref, d), rows(all_ref, me), i, d)

    def side_copy(i):
        d = peer(i)
        return remote(SIDE, side_out.at[d], lanes(side_all, me), i, d)

    def outgoing(kind, out_ref, dst_ref, i):
        d = source(i)
        return remote(kind, rows(out_ref, d), cols(dst_ref, me), i, d)

    def dp_copy(i):
        return pltpu.make_async_remote_copy(
            src_ref=mem_out,
            dst_ref=mem_dp.at[i],
            send_sem=dp_send.at[i],
            recv_sem=dp_recv.at[i],
            device_id={"dp": peer_dp(i)},
            device_id_type=MESH,
        )

    def tot_copy(i):
        return remote(MEM, tot_out, tot_all.at[me], i, peer(i))

    barrier = pltpu.get_barrier_semaphore()
    for i in range(1, n):
        pl.semaphore_signal(barrier, inc=1, device_id={"ctx": peer(i)}, device_id_type=MESH)
    for i in range(1, n_dp):
        pl.semaphore_signal(barrier, inc=1, device_id={"dp": peer_dp(i)}, device_id_type=MESH)

    if direct:
        product = do_ref[...].astype(F32) * o_ref[...].astype(F32)
        head_of = lax.broadcasted_iota(jnp.int32, (HEADS, HEADS * HDIM), 1) // HDIM
        row_of = lax.broadcasted_iota(jnp.int32, (HEADS, HEADS * HDIM), 0)
        pick = jnp.where(head_of == row_of, 1.0, 0.0).astype(BF16)
        high = product.astype(BF16)
        low = (product - high.astype(F32)).astype(BF16)
        delta = dot(pick, high, NT) + dot(pick, low, NT)
    row = lax.broadcasted_iota(jnp.int32, (total, tokens), 0)
    lane_block = lax.broadcasted_iota(jnp.int32, (total, tokens), 1) // BLK
    count = jnp.zeros((total, tokens), F32)
    for b in range(blocks):
        g = me * blocks + b
        here = lane_block == b
        named = [lax.rem(g + total - 1, total), g, lax.rem(g + 1, total)]
        named += [owner_ref[b, r] * blocks + local_ref[b, r] for r in range(per_block)]
        for j in named:
            count = count + jnp.where(here & (row == j), 1.0, 0.0)
    bias = jnp.where(count > 0, jnp.log(jnp.maximum(count, 1.0)), NONE)
    for d in range(n):
        side_out[d, :total, :] = bias
        side_out[d, total : total + heads, :] = lse_ref[d * heads : (d + 1) * heads, :]
        if direct:
            part = delta[d * heads : (d + 1) * heads, :]
        else:
            product = do_ref[d].astype(F32) * o_ref[d].astype(F32)
            one = jnp.ones((8, width), BF16)
            high = product.astype(BF16)
            low = (product - high.astype(F32)).astype(BF16)
            part = (dot(one, high, NT) + dot(one, low, NT))[:heads]
        side_out[d, total + heads : total + 2 * heads, :] = part

    pl.semaphore_wait(barrier, n - 1 + n_dp - 1)

    for i in range(1, n):
        incoming(Q, q_ref, q_all, i).start()
        incoming(DO, do_ref, do_all, i).start()
        side_copy(i).start()
    for i in range(1, n):
        incoming(K, k_ref, k_all, i).start()
        incoming(V, v_ref, v_all, i).start()
    rows(q_all, me)[...] = cols(q_ref, me)[...]
    rows(do_all, me)[...] = cols(do_ref, me)[...]
    rows(k_all, me)[...] = cols(k_ref, me)[...]
    rows(v_all, me)[...] = cols(v_ref, me)[...]
    lanes(side_all, me)[...] = side_out[me]
    for i in range(1, n):
        incoming(Q, q_ref, q_all, i).wait_recv()
        incoming(DO, do_ref, do_all, i).wait_recv()
        side_copy(i).wait_recv()

    q_all[...] = (q_all[...].astype(F32) * scale).astype(BF16)
    lane_head = lax.broadcasted_iota(jnp.int32, (1, width), 1) // HDIM

    def stacked(block):
        if heads == 1:
            return block
        return jnp.concatenate(
            [jnp.where(lane_head == h, block, jnp.zeros_like(block)) for h in range(heads)], axis=0
        )

    def merged(full, size):
        out = full[:size]
        for h in range(1, heads):
            out = jnp.where(lane_head == h, full[h * size : (h + 1) * size], out)
        return out

    def grads(key_blk, value_blk, shift):
        size = key_blk.shape[0]
        key_st, value_st = stacked(key_blk), stacked(value_blk)
        queries, douts = q_all[...], do_all[...]
        scores = dot(key_st, queries, NT)
        d_prob = dot(value_st, douts, NT)
        prob_parts, ds_parts = [], []
        for h in range(heads):
            delta_row = side_all[total + heads + h : total + heads + h + 1, :]
            step = size // len(shift[h])
            for b, shift_row in enumerate(shift[h]):
                lo = h * size + b * step
                prob = jnp.exp(scores[lo : lo + step] - shift_row)
                prob_parts.append(prob.astype(BF16))
                ds_parts.append((prob * (d_prob[lo : lo + step] - delta_row)).astype(BF16))
        prob_low = jnp.concatenate(prob_parts, axis=0)
        d_scores = jnp.concatenate(ds_parts, axis=0)
        grad_q = dot(key_st.T, d_scores, NN)
        grad_k = merged(dot(d_scores, queries, NN), size)
        grad_v = merged(dot(prob_low, douts, NN), size)
        return grad_q, grad_k, grad_v

    def lse_row(h):
        return side_all[total + h : total + h + 1, :]

    grad_q, grad_k, grad_v = grads(
        cols(gk_ref, me)[...], cols(gv_ref, me)[...], [[lse_row(h)] for h in range(heads)]
    )
    dq_sum[...] = grad_q
    mem_out[0] = grad_k.astype(BF16)
    mem_out[1] = grad_v.astype(BF16)
    for i in range(1, n_dp):
        dp_copy(i).start()

    def step(i):
        s = source(i)
        shift = [
            [lse_row(h) - side_all[pl.ds(s * blocks + b, 1), :] for b in range(blocks)]
            for h in range(heads)
        ]
        grad_q, grad_k, grad_v = grads(rows(k_all, s)[...], rows(v_all, s)[...], shift)
        dq_sum[...] += grad_q
        return grad_k.astype(BF16), grad_v.astype(BF16)

    def far_step(i, carry):
        incoming(K, k_ref, k_all, i).wait_recv()
        incoming(V, v_ref, v_all, i).wait_recv()
        grad_k, grad_v = step(i)
        s = source(i)
        rows(dk_out, s)[...] = grad_k
        rows(dv_out, s)[...] = grad_v
        outgoing(DK, dk_out, dk_ref, i).start()
        outgoing(DV, dv_out, dv_ref, i).start()
        return carry

    grad_k, grad_v = step(0)
    cols(dk_ref, me)[...] = grad_k
    cols(dv_ref, me)[...] = grad_v

    for i in range(1, n_dp):
        dp_copy(i).wait_recv()
    summed = mem_out[...].astype(F32)
    for i in range(1, n_dp):
        summed = summed + mem_dp[i].astype(F32)
    tot_out[...] = summed.astype(BF16)
    for i in range(1, n):
        tot_copy(i).start()
    cols(dgk_ref, me)[...] = tot_out[0].astype(F32)
    cols(dgv_ref, me)[...] = tot_out[1].astype(F32)

    lax.fori_loop(1, n, far_step, 0)

    dq_out[...] = (dq_sum[...].T * scale).astype(BF16)
    for i in range(1, n):
        outgoing(DQ, dq_out, dq_ref, i).start()
    cols(dq_ref, me)[...] = rows(dq_out, me)[...]

    for i in range(1, n):
        tot_copy(i).wait_recv()
        s = source(i)
        cols(dgk_ref, s)[...] = tot_all[s, 0].astype(F32)
        cols(dgv_ref, s)[...] = tot_all[s, 1].astype(F32)
    for i in range(1, n):
        outgoing(DK, dk_out, dk_ref, i).wait_recv()
        outgoing(DV, dv_out, dv_ref, i).wait_recv()
        outgoing(DQ, dq_out, dq_ref, i).wait_recv()
    for i in range(1, n):
        incoming(Q, q_ref, q_all, i).wait_send()
        incoming(DO, do_ref, do_all, i).wait_send()
        side_copy(i).wait_send()
        incoming(K, k_ref, k_all, i).wait_send()
        incoming(V, v_ref, v_all, i).wait_send()
        outgoing(DK, dk_out, dk_ref, i).wait_send()
        outgoing(DV, dv_out, dv_ref, i).wait_send()
        outgoing(DQ, dq_out, dq_ref, i).wait_send()
        tot_copy(i).wait_send()
    for i in range(1, n_dp):
        dp_copy(i).wait_send()


def shards(
    queries, keys, values, outputs, d_out, lse, glob_keys, glob_values, rand_owner, rand_local
):
    n = lax.axis_size("ctx")
    n_dp = lax.axis_size("dp")
    tokens = queries.shape[1]
    features = queries.shape[2]
    width = features // n
    heads = width // HDIM
    direct = width % 128 == 0
    total = n * (tokens // BLK)
    side_rows = -(-(total + 2 * heads) // 8) * 8

    def split(x):
        if direct:
            return x
        return x.reshape(x.shape[0], n, width).transpose(1, 0, 2)

    def join(x):
        if direct:
            return x
        return x.transpose(1, 0, 2).reshape(x.shape[1], features)

    def like(count, dtype):
        shape = (count, features) if direct else (n, count, width)
        return jax.ShapeDtypeStruct(shape, dtype)

    vmem = pl.BlockSpec(memory_space=pltpu.VMEM)
    smem = pl.BlockSpec(memory_space=pltpu.SMEM)
    whole = pltpu.VMEM((n * tokens, width), BF16)
    results = pl.pallas_call(
        functools.partial(kernel, n, n_dp, tokens, width, direct),
        out_shape=[like(tokens, BF16)] * 3 + [like(GLOB, F32)] * 2,
        in_specs=[smem] * 2 + [vmem] * 8,
        out_specs=[vmem] * 5,
        scratch_shapes=[
            whole,
            whole,
            whole,
            whole,
            pltpu.VMEM((n, side_rows, tokens), F32),
            pltpu.VMEM((side_rows, n * tokens), F32),
            whole,
            whole,
            whole,
            pltpu.VMEM((width, n * tokens), F32),
            pltpu.VMEM((2, GLOB, width), BF16),
            pltpu.VMEM((n_dp, 2, GLOB, width), BF16),
            pltpu.VMEM((2, GLOB, width), BF16),
            pltpu.VMEM((n, 2, GLOB, width), BF16),
            pltpu.SemaphoreType.DMA((9, n)),
            pltpu.SemaphoreType.DMA((9, n)),
            pltpu.SemaphoreType.DMA((n_dp,)),
            pltpu.SemaphoreType.DMA((n_dp,)),
        ],
        compiler_params=pltpu.CompilerParams(
            collective_id=0, has_side_effects=True, vmem_limit_bytes=48 * 1024 * 1024
        ),
    )(
        rand_owner,
        rand_local,
        split(queries[0]),
        split(keys[0]),
        split(values[0]),
        split(outputs[0]),
        split(d_out[0]),
        lse[0],
        split(glob_keys),
        split(glob_values),
    )
    dq, dk, dv, dgk, dgv = [join(x) for x in results]
    return dq[None], dk[None], dv[None], dgk, dgv


def solution(mesh):
    return jax.shard_map(
        shards,
        mesh=mesh,
        in_specs=(
            P("dp", "ctx", None),
            P("dp", "ctx", None),
            P("dp", "ctx", None),
            P("dp", "ctx", None),
            P("dp", "ctx", None),
            P("dp", None, "ctx"),
            P(),
            P(),
            P("ctx", None),
            P("ctx", None),
        ),
        out_specs=(P("dp", "ctx", None), P("dp", "ctx", None), P("dp", "ctx", None), P(), P()),
        check_vma=False,
    )
```

```python
import functools

import jax
import jax.numpy as jnp
from jax import lax
from jax.experimental import pallas as pl
from jax.experimental.pallas import tpu as pltpu
from jax.sharding import PartitionSpec as P

HEADS = 16
HDIM = 64
BLK = 64
GLOB = 128
NONE = -1e30
MESH = pl.DeviceIdType.MESH
F32 = jnp.float32
BF16 = jnp.bfloat16
NT = (((1,), (1,)), ((), ()))
NN = (((1,), (0,)), ((), ()))
Q, DO, SIDE, K, V, DK, DV, DQ, MEM = range(9)


def dot(a, b, dims):
    return lax.dot_general(a, b, dims, preferred_element_type=F32)


def kernel(
    n, n_dp, tokens, width, direct,
    owner_ref, local_ref, q_ref, k_ref, v_ref, o_ref, do_ref, lse_ref, gk_ref, gv_ref,
    dq_ref, dk_ref, dv_ref, tot_all,
    o_vm, do_vm, lse_vm, gk_vm, gv_vm, q_all, do_all, k_all, v_all, side_out, side_all, dq_out, dk_out, dv_out, dq_sum,
    mem_out, mem_dp, tot_out,
    send, recv, dp_send, dp_recv, own,
):
    me = lax.axis_index("ctx")
    me_dp = lax.axis_index("dp")
    heads = width // HDIM
    blocks = tokens // BLK
    total = n * blocks
    per_block = owner_ref.shape[1]
    scale = HDIM ** (-0.5)

    def peer(i):
        return lax.rem(me + i, n)

    def source(i):
        return lax.rem(me + n - i, n)

    def peer_dp(i):
        return lax.rem(me_dp + i, n_dp)

    def cols(ref, d):
        if direct:
            return ref.at[:, pl.ds(pl.multiple_of(d * width, width), width)]
        return ref.at[d]

    def rows(ref, d):
        return ref.at[pl.ds(pl.multiple_of(d * tokens, tokens), tokens), :]

    def lanes(ref, d):
        return ref.at[:, pl.ds(pl.multiple_of(d * tokens, tokens), tokens)]

    def remote(kind, src, dst, i, d):
        return pltpu.make_async_remote_copy(
            src_ref=src,
            dst_ref=dst,
            send_sem=send.at[kind, i],
            recv_sem=recv.at[kind, i],
            device_id={"ctx": d},
            device_id_type=MESH,
        )

    def incoming(kind, src_ref, all_ref, i):
        d = peer(i)
        return remote(kind, cols(src_ref, d), rows(all_ref, me), i, d)

    def side_copy(i):
        d = peer(i)
        return remote(SIDE, side_out.at[d], lanes(side_all, me), i, d)

    def outgoing(kind, out_ref, dst_ref, i):
        d = source(i)
        return remote(kind, rows(out_ref, d), cols(dst_ref, me), i, d)

    def dp_copy(i):
        return pltpu.make_async_remote_copy(
            src_ref=mem_out,
            dst_ref=mem_dp.at[i],
            send_sem=dp_send.at[i],
            recv_sem=dp_recv.at[i],
            device_id={"dp": peer_dp(i)},
            device_id_type=MESH,
        )

    def tot_copy(i):
        return remote(MEM, tot_out, tot_all.at[me], i, peer(i))

    barrier = pltpu.get_barrier_semaphore()
    for i in range(1, n):
        pl.semaphore_signal(barrier, inc=1, device_id={"ctx": peer(i)}, device_id_type=MESH)
    for i in range(1, n_dp):
        pl.semaphore_signal(barrier, inc=1, device_id={"dp": peer_dp(i)}, device_id_type=MESH)

    loads = [
        pltpu.make_async_copy(src, dst, own.at[i])
        for i, (src, dst) in enumerate(
            [
                (o_ref, o_vm),
                (do_ref, do_vm),
                (lse_ref, lse_vm),
                (cols(gk_ref, me), gk_vm),
                (cols(gv_ref, me), gv_vm),
                (cols(q_ref, me), rows(q_all, me)),
                (cols(do_ref, me), rows(do_all, me)),
                (cols(k_ref, me), rows(k_all, me)),
                (cols(v_ref, me), rows(v_all, me)),
            ]
        )
    ]
    for load in loads:
        load.start()
    for load in loads[:3]:
        load.wait()

    if direct:
        product = do_vm[...].astype(F32) * o_vm[...].astype(F32)
        head_of = lax.broadcasted_iota(jnp.int32, (HEADS, HEADS * HDIM), 1) // HDIM
        row_of = lax.broadcasted_iota(jnp.int32, (HEADS, HEADS * HDIM), 0)
        pick = jnp.where(head_of == row_of, 1.0, 0.0).astype(BF16)
        high = product.astype(BF16)
        low = (product - high.astype(F32)).astype(BF16)
        delta = dot(pick, high, NT) + dot(pick, low, NT)
    row = lax.broadcasted_iota(jnp.int32, (total, tokens), 0)
    lane_block = lax.broadcasted_iota(jnp.int32, (total, tokens), 1) // BLK
    count = jnp.zeros((total, tokens), F32)
    for b in range(blocks):
        g = me * blocks + b
        here = lane_block == b
        named = [lax.rem(g + total - 1, total), g, lax.rem(g + 1, total)]
        named += [owner_ref[b, r] * blocks + local_ref[b, r] for r in range(per_block)]
        for j in named:
            count = count + jnp.where(here & (row == j), 1.0, 0.0)
    bias = jnp.where(count > 0, jnp.log(jnp.maximum(count, 1.0)), NONE)
    for d in range(n):
        side_out[d, :total, :] = bias
        side_out[d, total : total + heads, :] = lse_vm[d * heads : (d + 1) * heads, :]
        if direct:
            part = delta[d * heads : (d + 1) * heads, :]
        else:
            product = do_vm[d].astype(F32) * o_vm[d].astype(F32)
            one = jnp.ones((8, width), BF16)
            high = product.astype(BF16)
            low = (product - high.astype(F32)).astype(BF16)
            part = (dot(one, high, NT) + dot(one, low, NT))[:heads]
        side_out[d, total + heads : total + 2 * heads, :] = part

    pl.semaphore_wait(barrier, n - 1 + n_dp - 1)

    for i in range(1, n):
        incoming(Q, q_ref, q_all, i).start()
        incoming(DO, do_ref, do_all, i).start()
        side_copy(i).start()
    for i in range(1, n):
        incoming(K, k_ref, k_all, i).start()
        incoming(V, v_ref, v_all, i).start()
    for load in loads[3:]:
        load.wait()
    lanes(side_all, me)[...] = side_out[me]
    for i in range(1, n):
        incoming(Q, q_ref, q_all, i).wait_recv()
        incoming(DO, do_ref, do_all, i).wait_recv()
        side_copy(i).wait_recv()

    q_all[...] = (q_all[...].astype(F32) * scale).astype(BF16)
    lane_head = lax.broadcasted_iota(jnp.int32, (1, width), 1) // HDIM

    def stacked(block):
        if heads == 1:
            return block
        return jnp.concatenate(
            [jnp.where(lane_head == h, block, jnp.zeros_like(block)) for h in range(heads)], axis=0
        )

    def merged(full, size):
        out = full[:size]
        for h in range(1, heads):
            out = jnp.where(lane_head == h, full[h * size : (h + 1) * size], out)
        return out

    def grads(key_blk, value_blk, shift):
        size = key_blk.shape[0]
        key_st, value_st = stacked(key_blk), stacked(value_blk)
        queries, douts = q_all[...], do_all[...]
        scores = dot(key_st, queries, NT)
        d_prob = dot(value_st, douts, NT)
        prob_parts, ds_parts = [], []
        for h in range(heads):
            delta_row = side_all[total + heads + h : total + heads + h + 1, :]
            step = size // len(shift[h])
            for b, shift_row in enumerate(shift[h]):
                lo = h * size + b * step
                prob = jnp.exp(scores[lo : lo + step] - shift_row)
                prob_parts.append(prob.astype(BF16))
                ds_parts.append((prob * (d_prob[lo : lo + step] - delta_row)).astype(BF16))
        prob_low = jnp.concatenate(prob_parts, axis=0)
        d_scores = jnp.concatenate(ds_parts, axis=0)
        grad_q = dot(key_st.T, d_scores, NN)
        grad_k = merged(dot(d_scores, queries, NN), size)
        grad_v = merged(dot(prob_low, douts, NN), size)
        return grad_q, grad_k, grad_v

    def lse_row(h):
        return side_all[total + h : total + h + 1, :]

    grad_q, grad_k, grad_v = grads(
        gk_vm[...], gv_vm[...], [[lse_row(h)] for h in range(heads)]
    )
    dq_sum[...] = grad_q
    mem_out[0] = grad_k.astype(BF16)
    mem_out[1] = grad_v.astype(BF16)
    for i in range(1, n_dp):
        dp_copy(i).start()

    def step(i):
        s = source(i)
        shift = [
            [lse_row(h) - side_all[pl.ds(s * blocks + b, 1), :] for b in range(blocks)]
            for h in range(heads)
        ]
        grad_q, grad_k, grad_v = grads(rows(k_all, s)[...], rows(v_all, s)[...], shift)
        dq_sum[...] += grad_q
        return grad_k.astype(BF16), grad_v.astype(BF16)

    def far_step(i, carry):
        incoming(K, k_ref, k_all, i).wait_recv()
        incoming(V, v_ref, v_all, i).wait_recv()
        grad_k, grad_v = step(i)
        s = source(i)
        rows(dk_out, s)[...] = grad_k
        rows(dv_out, s)[...] = grad_v
        outgoing(DK, dk_out, dk_ref, i).start()
        outgoing(DV, dv_out, dv_ref, i).start()
        return carry

    grad_k, grad_v = step(0)
    cols(dk_ref, me)[...] = grad_k
    cols(dv_ref, me)[...] = grad_v

    for i in range(1, n_dp):
        dp_copy(i).wait_recv()
    summed = mem_out[...].astype(F32)
    for i in range(1, n_dp):
        summed = summed + mem_dp[i].astype(F32)
    tot_out[...] = summed.astype(BF16)
    tot_all[me] = tot_out[...]
    for i in range(1, n):
        tot_copy(i).start()

    lax.fori_loop(1, n, far_step, 0)

    dq_out[...] = (dq_sum[...].T * scale).astype(BF16)
    for i in range(1, n):
        outgoing(DQ, dq_out, dq_ref, i).start()
    cols(dq_ref, me)[...] = rows(dq_out, me)[...]

    for i in range(1, n):
        tot_copy(i).wait_recv()
    for i in range(1, n):
        outgoing(DK, dk_out, dk_ref, i).wait_recv()
        outgoing(DV, dv_out, dv_ref, i).wait_recv()
        outgoing(DQ, dq_out, dq_ref, i).wait_recv()
    for i in range(1, n):
        incoming(Q, q_ref, q_all, i).wait_send()
        incoming(DO, do_ref, do_all, i).wait_send()
        side_copy(i).wait_send()
        incoming(K, k_ref, k_all, i).wait_send()
        incoming(V, v_ref, v_all, i).wait_send()
        outgoing(DK, dk_out, dk_ref, i).wait_send()
        outgoing(DV, dv_out, dv_ref, i).wait_send()
        outgoing(DQ, dq_out, dq_ref, i).wait_send()
        tot_copy(i).wait_send()
    for i in range(1, n_dp):
        dp_copy(i).wait_send()


def finish(
    n, width, direct, dq_ref, dk_ref, dv_ref, tot_ref,
    dq_out, dk_out, dv_out, dgk_out, dgv_out, dgk_vm, dgv_vm, sem,
):
    copies = [
        pltpu.make_async_copy(src, dst, sem.at[i])
        for i, (src, dst) in enumerate(
            [
                (dq_ref, dq_out),
                (dk_ref, dk_out),
                (dv_ref, dv_out),
                (dgk_vm, dgk_out),
                (dgv_vm, dgv_out),
            ]
        )
    ]
    for copy in copies[:3]:
        copy.start()
    for part, (vm, copy) in enumerate(zip((dgk_vm, dgv_vm), copies[3:])):
        for s in range(n):
            value = tot_ref[s, part].astype(F32)
            if direct:
                vm[:, s * width : (s + 1) * width] = value
            else:
                vm[s] = value
        copy.start()
    for copy in copies:
        copy.wait()


def shards(
    queries, keys, values, outputs, d_out, lse, glob_keys, glob_values, rand_owner, rand_local
):
    n = lax.axis_size("ctx")
    n_dp = lax.axis_size("dp")
    tokens = queries.shape[1]
    features = queries.shape[2]
    width = features // n
    heads = width // HDIM
    direct = width % 128 == 0
    total = n * (tokens // BLK)
    side_rows = -(-(total + 2 * heads) // 8) * 8

    def split(x):
        if direct:
            return x
        return x.reshape(x.shape[0], n, width).transpose(1, 0, 2)

    def join(x):
        if direct:
            return x
        return x.transpose(1, 0, 2).reshape(x.shape[1], features)

    def like(count, dtype):
        shape = (count, features) if direct else (n, count, width)
        return jax.ShapeDtypeStruct(shape, dtype)

    vmem = pl.BlockSpec(memory_space=pltpu.VMEM)
    hbm = pl.BlockSpec(memory_space=pltpu.HBM)
    smem = pl.BlockSpec(memory_space=pltpu.SMEM)
    whole = pltpu.VMEM((n * tokens, width), BF16)
    results = pl.pallas_call(
        functools.partial(kernel, n, n_dp, tokens, width, direct),
        out_shape=[like(tokens, BF16)] * 3
        + [jax.ShapeDtypeStruct((n, 2, GLOB, width), BF16)],
        in_specs=[smem] * 2 + [hbm] * 8,
        out_specs=[vmem] * 4,
        scratch_shapes=[
            pltpu.VMEM(like(tokens, BF16).shape, BF16),
            pltpu.VMEM(like(tokens, BF16).shape, BF16),
            pltpu.VMEM((HEADS, tokens), F32),
            pltpu.VMEM((GLOB, width), BF16),
            pltpu.VMEM((GLOB, width), BF16),
            whole,
            whole,
            whole,
            whole,
            pltpu.VMEM((n, side_rows, tokens), F32),
            pltpu.VMEM((side_rows, n * tokens), F32),
            whole,
            whole,
            whole,
            pltpu.VMEM((width, n * tokens), F32),
            pltpu.VMEM((2, GLOB, width), BF16),
            pltpu.VMEM((n_dp, 2, GLOB, width), BF16),
            pltpu.VMEM((2, GLOB, width), BF16),
            pltpu.SemaphoreType.DMA((9, n)),
            pltpu.SemaphoreType.DMA((9, n)),
            pltpu.SemaphoreType.DMA((n_dp,)),
            pltpu.SemaphoreType.DMA((n_dp,)),
            pltpu.SemaphoreType.DMA((9,)),
        ],
        compiler_params=pltpu.CompilerParams(
            collective_id=0, has_side_effects=True, vmem_limit_bytes=63 * 1024 * 1024
        ),
    )(
        rand_owner,
        rand_local,
        split(queries[0]),
        split(keys[0]),
        split(values[0]),
        split(outputs[0]),
        split(d_out[0]),
        lse[0],
        split(glob_keys),
        split(glob_values),
    )
    results = pl.pallas_call(
        functools.partial(finish, n, width, direct),
        out_shape=[like(tokens, BF16)] * 3 + [like(GLOB, F32)] * 2,
        in_specs=[hbm] * 3 + [vmem],
        out_specs=[hbm] * 5,
        scratch_shapes=[
            pltpu.VMEM(like(GLOB, F32).shape, F32),
            pltpu.VMEM(like(GLOB, F32).shape, F32),
            pltpu.SemaphoreType.DMA((5,)),
        ],
        compiler_params=pltpu.CompilerParams(vmem_limit_bytes=63 * 1024 * 1024),
    )(*results)
    dq, dk, dv, dgk, dgv = [join(x) for x in results]
    return dq[None], dk[None], dv[None], dgk, dgv


def solution(mesh):
    return jax.shard_map(
        shards,
        mesh=mesh,
        in_specs=(
            P("dp", "ctx", None),
            P("dp", "ctx", None),
            P("dp", "ctx", None),
            P("dp", "ctx", None),
            P("dp", "ctx", None),
            P("dp", None, "ctx"),
            P(),
            P(),
            P("ctx", None),
            P("ctx", None),
        ),
        out_specs=(P("dp", "ctx", None), P("dp", "ctx", None), P("dp", "ctx", None), P(), P()),
        check_vma=False,
    )
```

```python
import functools

import jax
import jax.numpy as jnp
from jax import lax
from jax.experimental import pallas as pl
from jax.experimental.pallas import tpu as pltpu
from jax.sharding import PartitionSpec as P

HEADS = 16
HDIM = 64
BLK = 64
GLOB = 128
NONE = -1e30
MESH = pl.DeviceIdType.MESH
F32 = jnp.float32
BF16 = jnp.bfloat16
NT = (((1,), (1,)), ((), ()))
NN = (((1,), (0,)), ((), ()))
Q, DO, SIDE, K, V, DK, DV, DQ, PART, CHIP, ALL_DP, CORE = range(12)


def dot(a, b, dims):
    return lax.dot_general(a, b, dims, preferred_element_type=F32)


def kernel(
    n, n_dp, tokens, width, direct,
    owner_ref, local_ref, q_ref, k_ref, v_ref, o_ref, do_ref, lse_ref, gk_ref, gv_ref,
    dq_ref, dk_ref, dv_ref, tot_all,
    o_vm, do_vm, lse_vm, gk_vm, gv_vm, q_all, do_all, k_all, v_all, side_out, side_all, dq_out, dk_out, dv_out, dq_sum,
    mem_out, mem_dp,
    send, recv, own,
):
    me = lax.axis_index("ctx")
    me_dp = lax.axis_index("dp")
    heads = width // HDIM
    blocks = tokens // BLK
    total = n * blocks
    per_block = owner_ref.shape[1]
    scale = HDIM ** (-0.5)

    def peer(i):
        return lax.rem(me + i, n)

    def source(i):
        return lax.rem(me + n - i, n)

    def peer_dp(i):
        return lax.rem(me_dp + i, n_dp)

    def cols(ref, d):
        if direct:
            return ref.at[:, pl.ds(pl.multiple_of(d * width, width), width)]
        return ref.at[d]

    def rows(ref, d):
        return ref.at[pl.ds(pl.multiple_of(d * tokens, tokens), tokens), :]

    def lanes(ref, d):
        return ref.at[:, pl.ds(pl.multiple_of(d * tokens, tokens), tokens)]

    def remote(kind, src, dst, i, d):
        return pltpu.make_async_remote_copy(
            src_ref=src,
            dst_ref=dst,
            send_sem=send.at[kind, i],
            recv_sem=recv.at[kind, i],
            device_id={"ctx": d},
            device_id_type=MESH,
        )

    def incoming(kind, src_ref, all_ref, i):
        d = peer(i)
        return remote(kind, cols(src_ref, d), rows(all_ref, me), i, d)

    def side_copy(i):
        d = peer(i)
        return remote(SIDE, side_out.at[d], lanes(side_all, me), i, d)

    def outgoing(kind, out_ref, dst_ref, i):
        d = source(i)
        return remote(kind, rows(out_ref, d), cols(dst_ref, me), i, d)

    core = lax.rem(me, 2)
    quarter = GLOB // n_dp

    def dp_remote(kind, src, dst, i):
        return pltpu.make_async_remote_copy(
            src_ref=src,
            dst_ref=dst,
            send_sem=send.at[kind, i],
            recv_sem=recv.at[kind, i],
            device_id={"dp": peer_dp(i)},
            device_id_type=MESH,
        )

    def part_copy(i):
        return dp_remote(PART, mem_out.at[peer_dp(i)], mem_dp.at[i], i)

    def chip_copy(i):
        block = tot_all.at[core, me_dp, me // 2]
        return remote(CHIP, block, block, i, peer(2 * i))

    def dp_copy(i):
        return dp_remote(ALL_DP, tot_all.at[core, me_dp], tot_all.at[core, me_dp], i)

    def core_copy():
        return remote(CORE, tot_all.at[core], tot_all.at[core], 0, me + 1 - 2 * core)

    barrier = pltpu.get_barrier_semaphore()
    for i in range(1, n):
        pl.semaphore_signal(barrier, inc=1, device_id={"ctx": peer(i)}, device_id_type=MESH)
    for i in range(1, n_dp):
        pl.semaphore_signal(barrier, inc=1, device_id={"dp": peer_dp(i)}, device_id_type=MESH)

    loads = [
        pltpu.make_async_copy(src, dst, own.at[i])
        for i, (src, dst) in enumerate(
            [
                (o_ref, o_vm),
                (do_ref, do_vm),
                (lse_ref, lse_vm),
                (cols(gk_ref, me), gk_vm),
                (cols(gv_ref, me), gv_vm),
                (cols(q_ref, me), rows(q_all, me)),
                (cols(do_ref, me), rows(do_all, me)),
                (cols(k_ref, me), rows(k_all, me)),
                (cols(v_ref, me), rows(v_all, me)),
            ]
        )
    ]
    for load in loads:
        load.start()
    pl.semaphore_wait(barrier, n - 1 + n_dp - 1)
    for i in range(1, n):
        incoming(Q, q_ref, q_all, i).start()
        incoming(DO, do_ref, do_all, i).start()
    for load in loads[:3]:
        load.wait()

    if direct:
        product = do_vm[...].astype(F32) * o_vm[...].astype(F32)
        head_of = lax.broadcasted_iota(jnp.int32, (HEADS, HEADS * HDIM), 1) // HDIM
        row_of = lax.broadcasted_iota(jnp.int32, (HEADS, HEADS * HDIM), 0)
        pick = jnp.where(head_of == row_of, 1.0, 0.0).astype(BF16)
        high = product.astype(BF16)
        low = (product - high.astype(F32)).astype(BF16)
        delta = dot(pick, high, NT) + dot(pick, low, NT)
    row = lax.broadcasted_iota(jnp.int32, (total, tokens), 0)
    lane_block = lax.broadcasted_iota(jnp.int32, (total, tokens), 1) // BLK
    count = jnp.zeros((total, tokens), F32)
    for b in range(blocks):
        g = me * blocks + b
        here = lane_block == b
        named = [lax.rem(g + total - 1, total), g, lax.rem(g + 1, total)]
        named += [owner_ref[b, r] * blocks + local_ref[b, r] for r in range(per_block)]
        for j in named:
            count = count + jnp.where(here & (row == j), 1.0, 0.0)
    bias = jnp.where(count > 0, jnp.log(jnp.maximum(count, 1.0)), NONE)
    for d in range(n):
        side_out[d, :total, :] = bias
        side_out[d, total : total + heads, :] = lse_vm[d * heads : (d + 1) * heads, :]
        if direct:
            part = delta[d * heads : (d + 1) * heads, :]
        else:
            product = do_vm[d].astype(F32) * o_vm[d].astype(F32)
            one = jnp.ones((8, width), BF16)
            high = product.astype(BF16)
            low = (product - high.astype(F32)).astype(BF16)
            part = (dot(one, high, NT) + dot(one, low, NT))[:heads]
        side_out[d, total + heads : total + 2 * heads, :] = part

    for i in range(1, n):
        side_copy(i).start()
    for i in range(1, n):
        incoming(K, k_ref, k_all, i).start()
        incoming(V, v_ref, v_all, i).start()
    for load in loads[3:]:
        load.wait()
    lanes(side_all, me)[...] = side_out[me]
    for i in range(1, n):
        incoming(Q, q_ref, q_all, i).wait_recv()
        incoming(DO, do_ref, do_all, i).wait_recv()
        side_copy(i).wait_recv()

    q_all[...] = (q_all[...].astype(F32) * scale).astype(BF16)
    lane_head = lax.broadcasted_iota(jnp.int32, (1, width), 1) // HDIM

    def stacked(block):
        if heads == 1:
            return block
        return jnp.concatenate(
            [jnp.where(lane_head == h, block, jnp.zeros_like(block)) for h in range(heads)], axis=0
        )

    def merged(full, size):
        out = full[:size]
        for h in range(1, heads):
            out = jnp.where(lane_head == h, full[h * size : (h + 1) * size], out)
        return out

    def grads(key_blk, value_blk, shift):
        size = key_blk.shape[0]
        key_st, value_st = stacked(key_blk), stacked(value_blk)
        queries, douts = q_all[...], do_all[...]
        scores = dot(key_st, queries, NT)
        d_prob = dot(value_st, douts, NT)
        prob_parts, ds_parts = [], []
        for h in range(heads):
            delta_row = side_all[total + heads + h : total + heads + h + 1, :]
            step = size // len(shift[h])
            for b, shift_row in enumerate(shift[h]):
                lo = h * size + b * step
                prob = jnp.exp(scores[lo : lo + step] - shift_row)
                prob_parts.append(prob.astype(BF16))
                ds_parts.append((prob * (d_prob[lo : lo + step] - delta_row)).astype(BF16))
        prob_low = jnp.concatenate(prob_parts, axis=0)
        d_scores = jnp.concatenate(ds_parts, axis=0)
        grad_q = dot(key_st.T, d_scores, NN)
        grad_k = merged(dot(d_scores, queries, NN), size)
        grad_v = merged(dot(prob_low, douts, NN), size)
        return grad_q, grad_k, grad_v

    def lse_row(h):
        return side_all[total + h : total + h + 1, :]

    grad_q, grad_k, grad_v = grads(
        gk_vm[...], gv_vm[...], [[lse_row(h)] for h in range(heads)]
    )
    dq_sum[...] = grad_q
    for p in range(n_dp):
        mem_out[p, 0] = grad_k[p * quarter : (p + 1) * quarter].astype(BF16)
        mem_out[p, 1] = grad_v[p * quarter : (p + 1) * quarter].astype(BF16)
    for i in range(1, n_dp):
        part_copy(i).start()

    def step(i):
        s = source(i)
        shift = [
            [lse_row(h) - side_all[pl.ds(s * blocks + b, 1), :] for b in range(blocks)]
            for h in range(heads)
        ]
        grad_q, grad_k, grad_v = grads(rows(k_all, s)[...], rows(v_all, s)[...], shift)
        dq_sum[...] += grad_q
        return grad_k.astype(BF16), grad_v.astype(BF16)

    def far_step(i, carry):
        incoming(K, k_ref, k_all, i).wait_recv()
        incoming(V, v_ref, v_all, i).wait_recv()
        @pl.when(i == 3)
        def _():
            for c in range(1, n // 2):
                chip_copy(c).wait_recv()
            for c in range(1, n_dp):
                dp_copy(c).start()

        grad_k, grad_v = step(i)
        s = source(i)
        rows(dk_out, s)[...] = grad_k
        rows(dv_out, s)[...] = grad_v
        outgoing(DK, dk_out, dk_ref, i).start()
        outgoing(DV, dv_out, dv_ref, i).start()
        return carry

    grad_k, grad_v = step(0)
    cols(dk_ref, me)[...] = grad_k
    cols(dv_ref, me)[...] = grad_v

    for i in range(1, n_dp):
        part_copy(i).wait_recv()
    summed = mem_out[me_dp].astype(F32)
    for i in range(1, n_dp):
        summed = summed + mem_dp[i].astype(F32)
    tot_all[core, me_dp, me // 2] = summed.astype(BF16)
    for i in range(1, n // 2):
        chip_copy(i).start()

    lax.fori_loop(1, n, far_step, 0)

    dq_out[...] = (dq_sum[...].T * scale).astype(BF16)
    for i in range(1, n):
        outgoing(DQ, dq_out, dq_ref, i).start()
    cols(dq_ref, me)[...] = rows(dq_out, me)[...]

    for i in range(1, n_dp):
        dp_copy(i).wait_recv()
    core_copy().start()
    core_copy().wait_recv()
    for i in range(1, n):
        outgoing(DK, dk_out, dk_ref, i).wait_recv()
        outgoing(DV, dv_out, dv_ref, i).wait_recv()
        outgoing(DQ, dq_out, dq_ref, i).wait_recv()
    for i in range(1, n):
        incoming(Q, q_ref, q_all, i).wait_send()
        incoming(DO, do_ref, do_all, i).wait_send()
        side_copy(i).wait_send()
        incoming(K, k_ref, k_all, i).wait_send()
        incoming(V, v_ref, v_all, i).wait_send()
        outgoing(DK, dk_out, dk_ref, i).wait_send()
        outgoing(DV, dv_out, dv_ref, i).wait_send()
        outgoing(DQ, dq_out, dq_ref, i).wait_send()
    for i in range(1, n_dp):
        part_copy(i).wait_send()
        dp_copy(i).wait_send()
    for i in range(1, n // 2):
        chip_copy(i).wait_send()
    core_copy().wait_send()


def finish(
    n, n_dp, width, direct, dq_ref, dk_ref, dv_ref, tot_ref,
    dq_out, dk_out, dv_out, dgk_out, dgv_out, dgk_vm, dgv_vm, sem,
):
    quarter = GLOB // n_dp
    copies = [
        pltpu.make_async_copy(src, dst, sem.at[i])
        for i, (src, dst) in enumerate(
            [
                (dq_ref, dq_out),
                (dk_ref, dk_out),
                (dv_ref, dv_out),
                (dgk_vm, dgk_out),
                (dgv_vm, dgv_out),
            ]
        )
    ]
    for copy in copies[:3]:
        copy.start()
    for part, (vm, copy) in enumerate(zip((dgk_vm, dgv_vm), copies[3:])):
        for s in range(n):
            for p in range(n_dp):
                value = tot_ref[s % 2, p, s // 2, part].astype(F32)
                rows = slice(p * quarter, (p + 1) * quarter)
                if direct:
                    vm[rows, s * width : (s + 1) * width] = value
                else:
                    vm[s, rows] = value
        copy.start()
    for copy in copies:
        copy.wait()


def shards(
    queries, keys, values, outputs, d_out, lse, glob_keys, glob_values, rand_owner, rand_local
):
    n = lax.axis_size("ctx")
    n_dp = lax.axis_size("dp")
    tokens = queries.shape[1]
    features = queries.shape[2]
    width = features // n
    heads = width // HDIM
    direct = width % 128 == 0
    total = n * (tokens // BLK)
    side_rows = -(-(total + 2 * heads) // 8) * 8

    def split(x):
        if direct:
            return x
        return x.reshape(x.shape[0], n, width).transpose(1, 0, 2)

    def join(x):
        if direct:
            return x
        return x.transpose(1, 0, 2).reshape(x.shape[1], features)

    def like(count, dtype):
        shape = (count, features) if direct else (n, count, width)
        return jax.ShapeDtypeStruct(shape, dtype)

    vmem = pl.BlockSpec(memory_space=pltpu.VMEM)
    hbm = pl.BlockSpec(memory_space=pltpu.HBM)
    smem = pl.BlockSpec(memory_space=pltpu.SMEM)
    whole = pltpu.VMEM((n * tokens, width), BF16)
    results = pl.pallas_call(
        functools.partial(kernel, n, n_dp, tokens, width, direct),
        out_shape=[pltpu.VMEM(like(tokens, BF16).shape, BF16)] * 3
        + [pltpu.VMEM((2, n_dp, n // 2, 2, GLOB // n_dp, width), BF16)],
        in_specs=[smem] * 2 + [hbm] * 8,
        out_specs=[vmem] * 4,
        scratch_shapes=[
            pltpu.VMEM(like(tokens, BF16).shape, BF16),
            pltpu.VMEM(like(tokens, BF16).shape, BF16),
            pltpu.VMEM((HEADS, tokens), F32),
            pltpu.VMEM((GLOB, width), BF16),
            pltpu.VMEM((GLOB, width), BF16),
            whole,
            whole,
            whole,
            whole,
            pltpu.VMEM((n, side_rows, tokens), F32),
            pltpu.VMEM((side_rows, n * tokens), F32),
            whole,
            whole,
            whole,
            pltpu.VMEM((width, n * tokens), F32),
            pltpu.VMEM((n_dp, 2, GLOB // n_dp, width), BF16),
            pltpu.VMEM((n_dp, 2, GLOB // n_dp, width), BF16),
            pltpu.SemaphoreType.DMA((12, max(n, n_dp))),
            pltpu.SemaphoreType.DMA((12, max(n, n_dp))),
            pltpu.SemaphoreType.DMA((9,)),
        ],
        compiler_params=pltpu.CompilerParams(
            collective_id=0, has_side_effects=True, vmem_limit_bytes=60 * 1024 * 1024
        ),
    )(
        rand_owner,
        rand_local,
        split(queries[0]),
        split(keys[0]),
        split(values[0]),
        split(outputs[0]),
        split(d_out[0]),
        lse[0],
        split(glob_keys),
        split(glob_values),
    )
    results = pl.pallas_call(
        functools.partial(finish, n, n_dp, width, direct),
        out_shape=[like(tokens, BF16)] * 3 + [like(GLOB, F32)] * 2,
        in_specs=[vmem] * 4,
        out_specs=[hbm] * 5,
        scratch_shapes=[
            pltpu.VMEM(like(GLOB, F32).shape, F32),
            pltpu.VMEM(like(GLOB, F32).shape, F32),
            pltpu.SemaphoreType.DMA((5,)),
        ],
        compiler_params=pltpu.CompilerParams(vmem_limit_bytes=16 * 1024 * 1024),
    )(*results)
    dq, dk, dv, dgk, dgv = [join(x) for x in results]
    return dq[None], dk[None], dv[None], dgk, dgv


def solution(mesh):
    return jax.shard_map(
        shards,
        mesh=mesh,
        in_specs=(
            P("dp", "ctx", None),
            P("dp", "ctx", None),
            P("dp", "ctx", None),
            P("dp", "ctx", None),
            P("dp", "ctx", None),
            P("dp", None, "ctx"),
            P(),
            P(),
            P("ctx", None),
            P("ctx", None),
        ),
        out_specs=(P("dp", "ctx", None), P("dp", "ctx", None), P("dp", "ctx", None), P(), P()),
        check_vma=False,
    )
```

```python
import functools

import jax
import jax.numpy as jnp
from jax import lax
from jax.experimental import pallas as pl
from jax.experimental.pallas import tpu as pltpu
from jax.sharding import PartitionSpec as P

HEADS = 16
HDIM = 64
BLK = 64
GLOB = 128
NONE = -1e30
MESH = pl.DeviceIdType.MESH
F32 = jnp.float32
BF16 = jnp.bfloat16
NT = (((1,), (1,)), ((), ()))
NN = (((1,), (0,)), ((), ()))
Q, DO, SIDE, K, V, DK, DV, DQ, PART, CHIP, ALL_DP, CORE = range(12)


def dot(a, b, dims):
    return lax.dot_general(a, b, dims, preferred_element_type=F32)


def kernel(
    n, n_dp, tokens, width, direct,
    owner_ref, local_ref, q_ref, k_ref, v_ref, o_ref, do_ref, lse_ref, gk_ref, gv_ref,
    dq_ref, dk_ref, dv_ref, tot_all,
    o_vm, do_vm, lse_vm, gk_vm, gv_vm, q_all, do_all, k_all, v_all, side_out, side_all, dq_out, dk_out, dv_out, dq_sum,
    mem_out, mem_dp, named_by, bias,
    send, recv, own,
):
    me = lax.axis_index("ctx")
    me_dp = lax.axis_index("dp")
    heads = width // HDIM
    blocks = tokens // BLK
    total = n * blocks
    per_block = owner_ref.shape[1]
    scale = HDIM ** (-0.5)

    def peer(i):
        return lax.rem(me + i, n)

    def source(i):
        return lax.rem(me + n - i, n)

    def peer_dp(i):
        return lax.rem(me_dp + i, n_dp)

    def cols(ref, d):
        if direct:
            return ref.at[:, pl.ds(pl.multiple_of(d * width, width), width)]
        return ref.at[d]

    def rows(ref, d):
        return ref.at[pl.ds(pl.multiple_of(d * tokens, tokens), tokens), :]

    def lanes(ref, d):
        return ref.at[:, pl.ds(pl.multiple_of(d * tokens, tokens), tokens)]

    def remote(kind, src, dst, i, d):
        return pltpu.make_async_remote_copy(
            src_ref=src,
            dst_ref=dst,
            send_sem=send.at[kind, i],
            recv_sem=recv.at[kind, i],
            device_id={"ctx": d},
            device_id_type=MESH,
        )

    def incoming(kind, src_ref, all_ref, i):
        d = peer(i)
        return remote(kind, cols(src_ref, d), rows(all_ref, me), i, d)

    def side_copy(i):
        d = peer(i)
        return remote(SIDE, side_out.at[d], lanes(side_all, me), i, d)

    def outgoing(kind, out_ref, dst_ref, i):
        d = source(i)
        return remote(kind, rows(out_ref, d), cols(dst_ref, me), i, d)

    core = lax.rem(me, 2)
    quarter = GLOB // n_dp

    def dp_remote(kind, src, dst, i):
        return pltpu.make_async_remote_copy(
            src_ref=src,
            dst_ref=dst,
            send_sem=send.at[kind, i],
            recv_sem=recv.at[kind, i],
            device_id={"dp": peer_dp(i)},
            device_id_type=MESH,
        )

    def part_copy(i):
        return dp_remote(PART, mem_out.at[peer_dp(i)], mem_dp.at[i], i)

    def chip_copy(i):
        block = tot_all.at[core, me_dp, me // 2]
        return remote(CHIP, block, block, i, peer(2 * i))

    def dp_copy(i):
        return dp_remote(ALL_DP, tot_all.at[core, me_dp], tot_all.at[core, me_dp], i)

    def core_copy():
        return remote(CORE, tot_all.at[core], tot_all.at[core], 0, me + 1 - 2 * core)

    barrier = pltpu.get_barrier_semaphore()
    for i in range(1, n):
        pl.semaphore_signal(barrier, inc=1, device_id={"ctx": peer(i)}, device_id_type=MESH)
    for i in range(1, n_dp):
        pl.semaphore_signal(barrier, inc=1, device_id={"dp": peer_dp(i)}, device_id_type=MESH)

    loads = [
        pltpu.make_async_copy(src, dst, own.at[i])
        for i, (src, dst) in enumerate(
            [
                (o_ref, o_vm),
                (do_ref, do_vm),
                (lse_ref, lse_vm),
                (cols(gk_ref, me), gk_vm),
                (cols(gv_ref, me), gv_vm),
                (cols(q_ref, me), rows(q_all, me)),
                (cols(do_ref, me), rows(do_all, me)),
                (cols(k_ref, me), rows(k_all, me)),
                (cols(v_ref, me), rows(v_all, me)),
            ]
        )
    ]
    for load in loads:
        load.start()
    pl.semaphore_wait(barrier, n - 1 + n_dp - 1)
    for i in range(1, n):
        incoming(Q, q_ref, q_all, i).start()
        incoming(DO, do_ref, do_all, i).start()
    for load in loads[:3]:
        load.wait()

    if direct:
        product = do_vm[...].astype(F32) * o_vm[...].astype(F32)
        head_of = lax.broadcasted_iota(jnp.int32, (HEADS, HEADS * HDIM), 1) // HDIM
        row_of = lax.broadcasted_iota(jnp.int32, (HEADS, HEADS * HDIM), 0)
        pick = jnp.where(head_of == row_of, 1.0, 0.0).astype(BF16)
        high = product.astype(BF16)
        low = (product - high.astype(F32)).astype(BF16)
        delta = dot(pick, high, NT) + dot(pick, low, NT)
    lane = lax.broadcasted_iota(jnp.int32, (1, tokens), 1)
    counts = []
    for b in range(blocks):
        g = me * blocks + b
        named = [lax.rem(g + total - 1, total), g, lax.rem(g + 1, total)]
        named += [owner_ref[b, r] * blocks + local_ref[b, r] for r in range(per_block)]
        count = jnp.zeros((1, tokens), F32)
        for j in named:
            count = count + jnp.where(lane == j, 1.0, 0.0)
        counts.append(count)
    for d in range(n):
        side_out[d, :heads, :] = lse_vm[d * heads : (d + 1) * heads, :]
        if direct:
            part = delta[d * heads : (d + 1) * heads, :]
        else:
            product = do_vm[d].astype(F32) * o_vm[d].astype(F32)
            one = jnp.ones((8, width), BF16)
            high = product.astype(BF16)
            low = (product - high.astype(F32)).astype(BF16)
            part = (dot(one, high, NT) + dot(one, low, NT))[:heads]
        side_out[d, heads : 2 * heads, :] = part
        for b in range(blocks):
            side_out[d, 2 * heads + b : 2 * heads + b + 1, :] = counts[b]

    for i in range(1, n):
        side_copy(i).start()
    for i in range(1, n):
        incoming(Q, q_ref, q_all, i).wait_send()
        incoming(DO, do_ref, do_all, i).wait_send()
    for i in range(1, n):
        incoming(K, k_ref, k_all, i).start()
        incoming(V, v_ref, v_all, i).start()
    for load in loads[3:]:
        load.wait()
    lanes(side_all, me)[...] = side_out[me]
    for i in range(1, n):
        incoming(Q, q_ref, q_all, i).wait_recv()
        incoming(DO, do_ref, do_all, i).wait_recv()
        side_copy(i).wait_recv()

    q_all[...] = (q_all[...].astype(F32) * scale).astype(BF16)
    lane_head = lax.broadcasted_iota(jnp.int32, (1, width), 1) // HDIM

    def stacked(block):
        if heads == 1:
            return block
        return jnp.concatenate(
            [jnp.where(lane_head == h, block, jnp.zeros_like(block)) for h in range(heads)], axis=0
        )

    def merged(full, size):
        out = full[:size]
        for h in range(1, heads):
            out = jnp.where(lane_head == h, full[h * size : (h + 1) * size], out)
        return out

    def grads(key_blk, value_blk, shift):
        size = key_blk.shape[0]
        key_st, value_st = stacked(key_blk), stacked(value_blk)
        queries, douts = q_all[...], do_all[...]
        scores = dot(key_st, queries, NT)
        d_prob = dot(value_st, douts, NT)
        prob_parts, ds_parts = [], []
        for h in range(heads):
            delta_row = side_all[heads + h : heads + h + 1, :]
            step = size // len(shift[h])
            for b, shift_row in enumerate(shift[h]):
                lo = h * size + b * step
                prob = jnp.exp(scores[lo : lo + step] - shift_row)
                prob_parts.append(prob.astype(BF16))
                ds_parts.append((prob * (d_prob[lo : lo + step] - delta_row)).astype(BF16))
        prob_low = jnp.concatenate(prob_parts, axis=0)
        d_scores = jnp.concatenate(ds_parts, axis=0)
        grad_q = dot(key_st.T, d_scores, NN)
        grad_k = merged(dot(d_scores, queries, NN), size)
        grad_v = merged(dot(prob_low, douts, NN), size)
        return grad_q, grad_k, grad_v

    def lse_row(h):
        return side_all[h : h + 1, :]

    grad_q, grad_k, grad_v = grads(
        gk_vm[...], gv_vm[...], [[lse_row(h)] for h in range(heads)]
    )
    dq_sum[...] = grad_q
    for p in range(n_dp):
        mem_out[p, 0] = grad_k[p * quarter : (p + 1) * quarter].astype(BF16)
        mem_out[p, 1] = grad_v[p * quarter : (p + 1) * quarter].astype(BF16)
    for i in range(1, n_dp):
        part_copy(i).start()

    for d in range(n):
        for b in range(blocks):
            named_by[d * blocks + b : d * blocks + b + 1, :] = side_all[
                2 * heads + b : 2 * heads + b + 1, d * tokens : (d + 1) * tokens
            ]
    block_of = lax.broadcasted_iota(jnp.int32, (total, n * tokens), 1) // BLK
    row_of = lax.broadcasted_iota(jnp.int32, (total, n * tokens), 0)
    spread = jnp.where(block_of == row_of, 1.0, 0.0).astype(BF16)
    count = dot(named_by[...].T.astype(BF16), spread, NN)[:total]
    bias[...] = jnp.where(count > 0, jnp.log(jnp.maximum(count, 1.0)), NONE)

    def step(i):
        s = source(i)
        shift = [
            [lse_row(h) - bias[pl.ds(s * blocks + b, 1), :] for b in range(blocks)]
            for h in range(heads)
        ]
        grad_q, grad_k, grad_v = grads(rows(k_all, s)[...], rows(v_all, s)[...], shift)
        dq_sum[...] += grad_q
        return grad_k.astype(BF16), grad_v.astype(BF16)

    def far_step(i, carry):
        incoming(K, k_ref, k_all, i).wait_recv()
        incoming(V, v_ref, v_all, i).wait_recv()
        @pl.when(i == 2)
        def _():
            for c in range(1, n_dp):
                part_copy(c).wait_recv()
            summed = mem_out[me_dp].astype(F32)
            for c in range(1, n_dp):
                summed = summed + mem_dp[c].astype(F32)
            tot_all[core, me_dp, me // 2] = summed.astype(BF16)
            for c in range(1, n // 2):
                chip_copy(c).start()

        @pl.when(i == 5)
        def _():
            for c in range(1, n // 2):
                chip_copy(c).wait_recv()
            for c in range(1, n_dp):
                dp_copy(c).start()

        grad_k, grad_v = step(i)
        s = source(i)
        rows(dk_out, s)[...] = grad_k
        rows(dv_out, s)[...] = grad_v
        outgoing(DK, dk_out, dk_ref, i).start()
        outgoing(DV, dv_out, dv_ref, i).start()
        return carry

    grad_k, grad_v = step(0)
    cols(dk_ref, me)[...] = grad_k
    cols(dv_ref, me)[...] = grad_v

    lax.fori_loop(1, n, far_step, 0)

    dq_out[...] = (dq_sum[...].T * scale).astype(BF16)
    for i in range(1, n):
        outgoing(DQ, dq_out, dq_ref, i).start()
    cols(dq_ref, me)[...] = rows(dq_out, me)[...]

    for i in range(1, n_dp):
        dp_copy(i).wait_recv()
    core_copy().start()
    core_copy().wait_recv()
    for i in range(1, n):
        outgoing(DK, dk_out, dk_ref, i).wait_recv()
        outgoing(DV, dv_out, dv_ref, i).wait_recv()
        outgoing(DQ, dq_out, dq_ref, i).wait_recv()
    for i in range(1, n):
        side_copy(i).wait_send()
        incoming(K, k_ref, k_all, i).wait_send()
        incoming(V, v_ref, v_all, i).wait_send()
        outgoing(DK, dk_out, dk_ref, i).wait_send()
        outgoing(DV, dv_out, dv_ref, i).wait_send()
        outgoing(DQ, dq_out, dq_ref, i).wait_send()
    for i in range(1, n_dp):
        part_copy(i).wait_send()
        dp_copy(i).wait_send()
    for i in range(1, n // 2):
        chip_copy(i).wait_send()
    core_copy().wait_send()


def finish(
    n, n_dp, width, direct, dq_ref, dk_ref, dv_ref, tot_ref,
    dq_out, dk_out, dv_out, dgk_out, dgv_out, dgk_vm, dgv_vm, sem,
):
    quarter = GLOB // n_dp
    copies = [
        pltpu.make_async_copy(src, dst, sem.at[i])
        for i, (src, dst) in enumerate(
            [
                (dq_ref, dq_out),
                (dk_ref, dk_out),
                (dv_ref, dv_out),
                (dgk_vm, dgk_out),
                (dgv_vm, dgv_out),
            ]
        )
    ]
    for copy in copies[:3]:
        copy.start()
    for part, (vm, copy) in enumerate(zip((dgk_vm, dgv_vm), copies[3:])):
        for s in range(n):
            for p in range(n_dp):
                value = tot_ref[s % 2, p, s // 2, part].astype(F32)
                rows = slice(p * quarter, (p + 1) * quarter)
                if direct:
                    vm[rows, s * width : (s + 1) * width] = value
                else:
                    vm[s, rows] = value
        copy.start()
    for copy in copies:
        copy.wait()


def shards(
    queries, keys, values, outputs, d_out, lse, glob_keys, glob_values, rand_owner, rand_local
):
    n = lax.axis_size("ctx")
    n_dp = lax.axis_size("dp")
    tokens = queries.shape[1]
    features = queries.shape[2]
    width = features // n
    heads = width // HDIM
    direct = width % 128 == 0
    total = n * (tokens // BLK)
    side_rows = -(-(2 * heads + tokens // BLK) // 8) * 8

    def split(x):
        if direct:
            return x
        return x.reshape(x.shape[0], n, width).transpose(1, 0, 2)

    def join(x):
        if direct:
            return x
        return x.transpose(1, 0, 2).reshape(x.shape[1], features)

    def like(count, dtype):
        shape = (count, features) if direct else (n, count, width)
        return jax.ShapeDtypeStruct(shape, dtype)

    vmem = pl.BlockSpec(memory_space=pltpu.VMEM)
    hbm = pl.BlockSpec(memory_space=pltpu.HBM)
    smem = pl.BlockSpec(memory_space=pltpu.SMEM)
    whole = pltpu.VMEM((n * tokens, width), BF16)
    results = pl.pallas_call(
        functools.partial(kernel, n, n_dp, tokens, width, direct),
        out_shape=[pltpu.VMEM(like(tokens, BF16).shape, BF16)] * 3
        + [pltpu.VMEM((2, n_dp, n // 2, 2, GLOB // n_dp, width), BF16)],
        in_specs=[smem] * 2 + [hbm] * 8,
        out_specs=[vmem] * 4,
        scratch_shapes=[
            pltpu.VMEM(like(tokens, BF16).shape, BF16),
            pltpu.VMEM(like(tokens, BF16).shape, BF16),
            pltpu.VMEM((HEADS, tokens), F32),
            pltpu.VMEM((GLOB, width), BF16),
            pltpu.VMEM((GLOB, width), BF16),
            whole,
            whole,
            whole,
            whole,
            pltpu.VMEM((n, side_rows, tokens), F32),
            pltpu.VMEM((side_rows, n * tokens), F32),
            whole,
            whole,
            whole,
            pltpu.VMEM((width, n * tokens), F32),
            pltpu.VMEM((n_dp, 2, GLOB // n_dp, width), BF16),
            pltpu.VMEM((n_dp, 2, GLOB // n_dp, width), BF16),
            pltpu.VMEM((total, tokens), F32),
            pltpu.VMEM((total, n * tokens), F32),
            pltpu.SemaphoreType.DMA((12, max(n, n_dp))),
            pltpu.SemaphoreType.DMA((12, max(n, n_dp))),
            pltpu.SemaphoreType.DMA((9,)),
        ],
        compiler_params=pltpu.CompilerParams(
            collective_id=0, has_side_effects=True, vmem_limit_bytes=60 * 1024 * 1024
        ),
    )(
        rand_owner,
        rand_local,
        split(queries[0]),
        split(keys[0]),
        split(values[0]),
        split(outputs[0]),
        split(d_out[0]),
        lse[0],
        split(glob_keys),
        split(glob_values),
    )
    results = pl.pallas_call(
        functools.partial(finish, n, n_dp, width, direct),
        out_shape=[like(tokens, BF16)] * 3 + [like(GLOB, F32)] * 2,
        in_specs=[vmem] * 4,
        out_specs=[hbm] * 5,
        scratch_shapes=[
            pltpu.VMEM(like(GLOB, F32).shape, F32),
            pltpu.VMEM(like(GLOB, F32).shape, F32),
            pltpu.SemaphoreType.DMA((5,)),
        ],
        compiler_params=pltpu.CompilerParams(vmem_limit_bytes=16 * 1024 * 1024),
    )(*results)
    dq, dk, dv, dgk, dgv = [join(x) for x in results]
    return dq[None], dk[None], dv[None], dgk, dgv


def solution(mesh):
    return jax.shard_map(
        shards,
        mesh=mesh,
        in_specs=(
            P("dp", "ctx", None),
            P("dp", "ctx", None),
            P("dp", "ctx", None),
            P("dp", "ctx", None),
            P("dp", "ctx", None),
            P("dp", None, "ctx"),
            P(),
            P(),
            P("ctx", None),
            P("ctx", None),
        ),
        out_specs=(P("dp", "ctx", None), P("dp", "ctx", None), P("dp", "ctx", None), P(), P()),
        check_vma=False,
    )
```

```python
import functools

import jax
import jax.numpy as jnp
from jax import lax
from jax.experimental import pallas as pl
from jax.experimental.pallas import tpu as pltpu
from jax.sharding import PartitionSpec as P

HEADS = 16
HDIM = 64
BLK = 64
GLOB = 128
NONE = -1e30
MESH = pl.DeviceIdType.MESH
F32 = jnp.float32
BF16 = jnp.bfloat16
NT = (((1,), (1,)), ((), ()))
NN = (((1,), (0,)), ((), ()))
Q, DO, SIDE, K, V, DK, DV, DQ, PART, CHIP, ALL_DP, CORE = range(12)


def dot(a, b, dims):
    return lax.dot_general(a, b, dims, preferred_element_type=F32)


def kernel(
    n, n_dp, tokens, width, direct,
    owner_ref, local_ref, q_ref, k_ref, v_ref, o_ref, do_ref, lse_ref, gk_ref, gv_ref,
    dq_ref, dk_ref, dv_ref, tot_all,
    o_vm, do_vm, lse_vm, gk_vm, gv_vm, q_all, do_all, k_all, v_all, side_out, side_all, dq_out, dk_out, dv_out, dq_sum,
    mem_out, mem_dp, named_by, bias,
    send, recv, own,
):
    me = lax.axis_index("ctx")
    me_dp = lax.axis_index("dp")
    heads = width // HDIM
    blocks = tokens // BLK
    total = n * blocks
    per_block = owner_ref.shape[1]
    scale = HDIM ** (-0.5)

    def peer(i):
        return lax.rem(me + i, n)

    def source(i):
        return lax.rem(me + n - i, n)

    def peer_dp(i):
        return lax.rem(me_dp + i, n_dp)

    def cols(ref, d):
        if direct:
            return ref.at[:, pl.ds(pl.multiple_of(d * width, width), width)]
        return ref.at[d]

    def rows(ref, d):
        return ref.at[pl.ds(pl.multiple_of(d * tokens, tokens), tokens), :]

    def lanes(ref, d):
        return ref.at[:, pl.ds(pl.multiple_of(d * tokens, tokens), tokens)]

    def remote(kind, src, dst, i, d):
        return pltpu.make_async_remote_copy(
            src_ref=src,
            dst_ref=dst,
            send_sem=send.at[kind, i],
            recv_sem=recv.at[kind, i],
            device_id={"ctx": d},
            device_id_type=MESH,
        )

    def incoming(kind, src_ref, all_ref, i):
        d = peer(i)
        return remote(kind, cols(src_ref, d), rows(all_ref, me), i, d)

    def side_copy(i):
        d = peer(i)
        return remote(SIDE, side_out.at[d], lanes(side_all, me), i, d)

    def outgoing(kind, out_ref, dst_ref, i):
        d = source(i)
        return remote(kind, rows(out_ref, d), cols(dst_ref, me), i, d)

    core = lax.rem(me, 2)
    quarter = GLOB // n_dp

    def dp_remote(kind, src, dst, i):
        return pltpu.make_async_remote_copy(
            src_ref=src,
            dst_ref=dst,
            send_sem=send.at[kind, i],
            recv_sem=recv.at[kind, i],
            device_id={"dp": peer_dp(i)},
            device_id_type=MESH,
        )

    def part_copy(i):
        return dp_remote(PART, mem_out.at[peer_dp(i)], mem_dp.at[i], i)

    def chip_copy(i):
        block = tot_all.at[core, me_dp, me // 2]
        return remote(CHIP, block, block, i, peer(2 * i))

    def dp_copy(i):
        return dp_remote(ALL_DP, tot_all.at[core, me_dp], tot_all.at[core, me_dp], i)

    def core_copy(i):
        block = tot_all.at[core, lax.rem(me_dp + n_dp - i, n_dp)]
        return remote(CORE, block, block, i, me + 1 - 2 * core)

    barrier = pltpu.get_barrier_semaphore()
    for i in range(1, n):
        pl.semaphore_signal(barrier, inc=1, device_id={"ctx": peer(i)}, device_id_type=MESH)
    for i in range(1, n_dp):
        pl.semaphore_signal(barrier, inc=1, device_id={"dp": peer_dp(i)}, device_id_type=MESH)

    loads = [
        pltpu.make_async_copy(src, dst, own.at[i])
        for i, (src, dst) in enumerate(
            [
                (o_ref, o_vm),
                (do_ref, do_vm),
                (lse_ref, lse_vm),
                (cols(gk_ref, me), gk_vm),
                (cols(gv_ref, me), gv_vm),
                (cols(q_ref, me), rows(q_all, me)),
                (cols(do_ref, me), rows(do_all, me)),
                (cols(k_ref, me), rows(k_all, me)),
                (cols(v_ref, me), rows(v_all, me)),
            ]
        )
    ]
    for load in loads:
        load.start()
    pl.semaphore_wait(barrier, n - 1 + n_dp - 1)
    for i in range(1, n):
        incoming(Q, q_ref, q_all, i).start()
        incoming(DO, do_ref, do_all, i).start()
    for load in loads[:3]:
        load.wait()

    if direct:
        product = do_vm[...].astype(F32) * o_vm[...].astype(F32)
        head_of = lax.broadcasted_iota(jnp.int32, (HEADS, HEADS * HDIM), 1) // HDIM
        row_of = lax.broadcasted_iota(jnp.int32, (HEADS, HEADS * HDIM), 0)
        pick = jnp.where(head_of == row_of, 1.0, 0.0).astype(BF16)
        high = product.astype(BF16)
        low = (product - high.astype(F32)).astype(BF16)
        delta = dot(pick, high, NT) + dot(pick, low, NT)
    lane = lax.broadcasted_iota(jnp.int32, (1, tokens), 1)
    counts = []
    for b in range(blocks):
        g = me * blocks + b
        named = [lax.rem(g + total - 1, total), g, lax.rem(g + 1, total)]
        named += [owner_ref[b, r] * blocks + local_ref[b, r] for r in range(per_block)]
        count = jnp.zeros((1, tokens), F32)
        for j in named:
            count = count + jnp.where(lane == j, 1.0, 0.0)
        counts.append(count)
    for d in range(n):
        side_out[d, :heads, :] = lse_vm[d * heads : (d + 1) * heads, :]
        if direct:
            part = delta[d * heads : (d + 1) * heads, :]
        else:
            product = do_vm[d].astype(F32) * o_vm[d].astype(F32)
            one = jnp.ones((8, width), BF16)
            high = product.astype(BF16)
            low = (product - high.astype(F32)).astype(BF16)
            part = (dot(one, high, NT) + dot(one, low, NT))[:heads]
        side_out[d, heads : 2 * heads, :] = part
        for b in range(blocks):
            side_out[d, 2 * heads + b : 2 * heads + b + 1, :] = counts[b]

    for i in range(1, n):
        side_copy(i).start()
    for i in range(1, n):
        incoming(Q, q_ref, q_all, i).wait_send()
        incoming(DO, do_ref, do_all, i).wait_send()
    for i in range(1, n):
        incoming(K, k_ref, k_all, i).start()
        incoming(V, v_ref, v_all, i).start()
    for load in loads[3:]:
        load.wait()
    lanes(side_all, me)[...] = side_out[me]
    for i in range(1, n):
        incoming(Q, q_ref, q_all, i).wait_recv()
        incoming(DO, do_ref, do_all, i).wait_recv()
        side_copy(i).wait_recv()

    q_all[...] = (q_all[...].astype(F32) * scale).astype(BF16)
    lane_head = lax.broadcasted_iota(jnp.int32, (1, width), 1) // HDIM

    def stacked(block):
        if heads == 1:
            return block
        return jnp.concatenate(
            [jnp.where(lane_head == h, block, jnp.zeros_like(block)) for h in range(heads)], axis=0
        )

    def merged(full, size):
        out = full[:size]
        for h in range(1, heads):
            out = jnp.where(lane_head == h, full[h * size : (h + 1) * size], out)
        return out

    def grads(key_blk, value_blk, shift):
        size = key_blk.shape[0]
        key_st, value_st = stacked(key_blk), stacked(value_blk)
        queries, douts = q_all[...], do_all[...]
        scores = dot(key_st, queries, NT)
        d_prob = dot(value_st, douts, NT)
        prob_parts, ds_parts = [], []
        for h in range(heads):
            delta_row = side_all[heads + h : heads + h + 1, :]
            step = size // len(shift[h])
            for b, shift_row in enumerate(shift[h]):
                lo = h * size + b * step
                prob = jnp.exp(scores[lo : lo + step] - shift_row)
                prob_parts.append(prob.astype(BF16))
                ds_parts.append((prob * (d_prob[lo : lo + step] - delta_row)).astype(BF16))
        prob_low = jnp.concatenate(prob_parts, axis=0)
        d_scores = jnp.concatenate(ds_parts, axis=0)
        grad_q = dot(key_st.T, d_scores, NN)
        grad_k = merged(dot(d_scores, queries, NN), size)
        grad_v = merged(dot(prob_low, douts, NN), size)
        return grad_q, grad_k, grad_v

    def lse_row(h):
        return side_all[h : h + 1, :]

    grad_q, grad_k, grad_v = grads(
        gk_vm[...], gv_vm[...], [[lse_row(h)] for h in range(heads)]
    )
    dq_sum[...] = grad_q
    for p in range(n_dp):
        mem_out[p, 0] = grad_k[p * quarter : (p + 1) * quarter].astype(BF16)
        mem_out[p, 1] = grad_v[p * quarter : (p + 1) * quarter].astype(BF16)
    for i in range(1, n_dp):
        part_copy(i).start()

    for d in range(n):
        for b in range(blocks):
            named_by[d * blocks + b : d * blocks + b + 1, :] = side_all[
                2 * heads + b : 2 * heads + b + 1, d * tokens : (d + 1) * tokens
            ]
    block_of = lax.broadcasted_iota(jnp.int32, (total, n * tokens), 1) // BLK
    row_of = lax.broadcasted_iota(jnp.int32, (total, n * tokens), 0)
    spread = jnp.where(block_of == row_of, 1.0, 0.0).astype(BF16)
    count = dot(named_by[...].T.astype(BF16), spread, NN)[:total]
    bias[...] = jnp.where(count > 0, jnp.log(jnp.maximum(count, 1.0)), NONE)

    def step(i):
        s = source(i)
        shift = [
            [lse_row(h) - bias[pl.ds(s * blocks + b, 1), :] for b in range(blocks)]
            for h in range(heads)
        ]
        grad_q, grad_k, grad_v = grads(rows(k_all, s)[...], rows(v_all, s)[...], shift)
        dq_sum[...] += grad_q
        return grad_k.astype(BF16), grad_v.astype(BF16)

    def far_step(i, carry):
        incoming(K, k_ref, k_all, i).wait_recv()
        incoming(V, v_ref, v_all, i).wait_recv()
        @pl.when(i == 2)
        def _():
            for c in range(1, n_dp):
                part_copy(c).wait_recv()
            summed = mem_out[me_dp].astype(F32)
            for c in range(1, n_dp):
                summed = summed + mem_dp[c].astype(F32)
            tot_all[core, me_dp, me // 2] = summed.astype(BF16)
            for c in range(1, n // 2):
                chip_copy(c).start()

        @pl.when(i == 5)
        def _():
            for c in range(1, n // 2):
                chip_copy(c).wait_recv()
            for c in range(1, n_dp):
                dp_copy(c).start()
            core_copy(0).start()

        grad_k, grad_v = step(i)
        s = source(i)
        rows(dk_out, s)[...] = grad_k
        rows(dv_out, s)[...] = grad_v
        outgoing(DK, dk_out, dk_ref, i).start()
        outgoing(DV, dv_out, dv_ref, i).start()
        return carry

    grad_k, grad_v = step(0)
    cols(dk_ref, me)[...] = grad_k
    cols(dv_ref, me)[...] = grad_v

    lax.fori_loop(1, n, far_step, 0)

    dq_out[...] = (dq_sum[...].T * scale).astype(BF16)
    for i in range(1, n):
        outgoing(DQ, dq_out, dq_ref, i).start()
    cols(dq_ref, me)[...] = rows(dq_out, me)[...]

    for i in range(1, n_dp):
        dp_copy(i).wait_recv()
        core_copy(i).start()
    for i in range(n_dp):
        core_copy(i).wait_recv()
    for i in range(1, n):
        outgoing(DK, dk_out, dk_ref, i).wait_recv()
        outgoing(DV, dv_out, dv_ref, i).wait_recv()
        outgoing(DQ, dq_out, dq_ref, i).wait_recv()
    for i in range(1, n):
        side_copy(i).wait_send()
        incoming(K, k_ref, k_all, i).wait_send()
        incoming(V, v_ref, v_all, i).wait_send()
        outgoing(DK, dk_out, dk_ref, i).wait_send()
        outgoing(DV, dv_out, dv_ref, i).wait_send()
        outgoing(DQ, dq_out, dq_ref, i).wait_send()
    for i in range(1, n_dp):
        part_copy(i).wait_send()
        dp_copy(i).wait_send()
    for i in range(1, n // 2):
        chip_copy(i).wait_send()
    for i in range(n_dp):
        core_copy(i).wait_send()


def finish(
    n, n_dp, width, direct, dq_ref, dk_ref, dv_ref, tot_ref,
    dq_out, dk_out, dv_out, dgk_out, dgv_out, dgk_vm, dgv_vm, sem,
):
    quarter = GLOB // n_dp
    copies = [
        pltpu.make_async_copy(src, dst, sem.at[i])
        for i, (src, dst) in enumerate(
            [
                (dq_ref, dq_out),
                (dk_ref, dk_out),
                (dv_ref, dv_out),
                (dgk_vm, dgk_out),
                (dgv_vm, dgv_out),
            ]
        )
    ]
    for copy in copies[:3]:
        copy.start()
    for part, (vm, copy) in enumerate(zip((dgk_vm, dgv_vm), copies[3:])):
        for s in range(n):
            for p in range(n_dp):
                value = tot_ref[s % 2, p, s // 2, part].astype(F32)
                rows = slice(p * quarter, (p + 1) * quarter)
                if direct:
                    vm[rows, s * width : (s + 1) * width] = value
                else:
                    vm[s, rows] = value
        copy.start()
    for copy in copies:
        copy.wait()


def shards(
    queries, keys, values, outputs, d_out, lse, glob_keys, glob_values, rand_owner, rand_local
):
    n = lax.axis_size("ctx")
    n_dp = lax.axis_size("dp")
    tokens = queries.shape[1]
    features = queries.shape[2]
    width = features // n
    heads = width // HDIM
    direct = width % 128 == 0
    total = n * (tokens // BLK)
    side_rows = -(-(2 * heads + tokens // BLK) // 8) * 8

    def split(x):
        if direct:
            return x
        return x.reshape(x.shape[0], n, width).transpose(1, 0, 2)

    def join(x):
        if direct:
            return x
        return x.transpose(1, 0, 2).reshape(x.shape[1], features)

    def like(count, dtype):
        shape = (count, features) if direct else (n, count, width)
        return jax.ShapeDtypeStruct(shape, dtype)

    vmem = pl.BlockSpec(memory_space=pltpu.VMEM)
    hbm = pl.BlockSpec(memory_space=pltpu.HBM)
    smem = pl.BlockSpec(memory_space=pltpu.SMEM)
    whole = pltpu.VMEM((n * tokens, width), BF16)
    results = pl.pallas_call(
        functools.partial(kernel, n, n_dp, tokens, width, direct),
        out_shape=[pltpu.VMEM(like(tokens, BF16).shape, BF16)] * 3
        + [pltpu.VMEM((2, n_dp, n // 2, 2, GLOB // n_dp, width), BF16)],
        in_specs=[smem] * 2 + [hbm] * 8,
        out_specs=[vmem] * 4,
        scratch_shapes=[
            pltpu.VMEM(like(tokens, BF16).shape, BF16),
            pltpu.VMEM(like(tokens, BF16).shape, BF16),
            pltpu.VMEM((HEADS, tokens), F32),
            pltpu.VMEM((GLOB, width), BF16),
            pltpu.VMEM((GLOB, width), BF16),
            whole,
            whole,
            whole,
            whole,
            pltpu.VMEM((n, side_rows, tokens), F32),
            pltpu.VMEM((side_rows, n * tokens), F32),
            whole,
            whole,
            whole,
            pltpu.VMEM((width, n * tokens), F32),
            pltpu.VMEM((n_dp, 2, GLOB // n_dp, width), BF16),
            pltpu.VMEM((n_dp, 2, GLOB // n_dp, width), BF16),
            pltpu.VMEM((total, tokens), F32),
            pltpu.VMEM((total, n * tokens), F32),
            pltpu.SemaphoreType.DMA((12, max(n, n_dp))),
            pltpu.SemaphoreType.DMA((12, max(n, n_dp))),
            pltpu.SemaphoreType.DMA((9,)),
        ],
        compiler_params=pltpu.CompilerParams(
            collective_id=0, has_side_effects=True, vmem_limit_bytes=60 * 1024 * 1024
        ),
    )(
        rand_owner,
        rand_local,
        split(queries[0]),
        split(keys[0]),
        split(values[0]),
        split(outputs[0]),
        split(d_out[0]),
        lse[0],
        split(glob_keys),
        split(glob_values),
    )
    results = pl.pallas_call(
        functools.partial(finish, n, n_dp, width, direct),
        out_shape=[like(tokens, BF16)] * 3 + [like(GLOB, F32)] * 2,
        in_specs=[vmem] * 4,
        out_specs=[hbm] * 5,
        scratch_shapes=[
            pltpu.VMEM(like(GLOB, F32).shape, F32),
            pltpu.VMEM(like(GLOB, F32).shape, F32),
            pltpu.SemaphoreType.DMA((5,)),
        ],
        compiler_params=pltpu.CompilerParams(vmem_limit_bytes=16 * 1024 * 1024),
    )(*results)
    dq, dk, dv, dgk, dgv = [join(x) for x in results]
    return dq[None], dk[None], dv[None], dgk, dgv


def solution(mesh):
    return jax.shard_map(
        shards,
        mesh=mesh,
        in_specs=(
            P("dp", "ctx", None),
            P("dp", "ctx", None),
            P("dp", "ctx", None),
            P("dp", "ctx", None),
            P("dp", "ctx", None),
            P("dp", None, "ctx"),
            P(),
            P(),
            P("ctx", None),
            P("ctx", None),
        ),
        out_specs=(P("dp", "ctx", None), P("dp", "ctx", None), P("dp", "ctx", None), P(), P()),
        check_vma=False,
    )
```
